256 devices in a mesh: seq: 8 (over z_hi, x), exp: 32 (over z_lo, y, core).
Axes of the slice: x: 4, y: 4, z: 8 (z_hi: 2, z_lo: 4; z = z_hi * 4 + z_lo), core: 2. Of those that a mesh axis runs over, the one named last changes fastest.
Arguments:
- tokens: bfloat16 [8192, 1664], P('seq'), may hold values from -6 to 6
- out_grad: bfloat16 [8192, 1664], P('seq'), may hold values from -6 to 6
- slot_params: bfloat16 [1024, 1664], P('exp'), may hold values from -6 to 6
- first_mixing: float32 [64, 4, 4, 4], P('exp'), may hold values from -3 to 3
- first_blocks: bfloat16 [64, 4, 416, 2048], P('exp', None, None, 'seq'), may hold values from -0.15625 to 0.15625
- second_mixing: float32 [64, 4, 4, 4], P('exp'), may hold values from -3 to 3
- second_blocks: bfloat16 [64, 4, 2048, 416], P('exp', None, 'seq'), may hold values from -0.0625 to 0.0625
Outputs:
- grad_tokens: float32 [8192, 1664], P(('seq', 'exp'))
- grad_slots: float32 [1024, 1664], P('exp')
- grad_first_mixing: float32 [64, 4, 4, 4], P('exp')
- grad_first_blocks: bfloat16 [64, 4, 416, 2048], P('exp', None, None, 'seq')
- grad_second_mixing: float32 [64, 4, 4, 4], P('exp')
- grad_second_blocks: bfloat16 [64, 4, 2048, 416], P('exp', None, 'seq')
The draws below stay inside these ranges and needn't reach their ends.
All inputs are finite; a program needn't handle non-finite values.
Results may differ from the reference program's by a relative error of at most 0.04.
Values may be sent and summed in bfloat16 or wider, within the bound.
No kernel may reach another device: no remote copies, remote signals or barrier semaphores. Data moves between devices by JAX's collectives and lax.ppermute only.
A program may use at most 128 MiB of HBM per device.

```python
import jax
import jax.numpy as jnp
from jax import lax

D = 1664
HID = 8192
N_PHM = 4
SLOTS = 16
TOKENS = 8192
EXPERTS = 64
SLOT_ALL = 1024
DB = 416
HBLOCK = 2048


def block_scale(key, shape, pieces, smallest, top_value):
    def one(dim, blocks):
        heights = jax.random.uniform(jax.random.fold_in(jax.random.fold_in(key, 6), dim), (blocks,), jnp.float32, smallest / len(pieces), top_value / len(pieces))
        return jnp.repeat(jnp.exp(heights), shape[dim] // blocks).reshape((-1,) + (1,) * (len(shape) - dim - 1))

    level = one(*pieces[0])
    for cut in pieces[1:]:
        level = level * one(*cut)
    return level


def bell_draw(rng, shape, spread, bound, split=(), held_as=jnp.bfloat16):
    loudness = block_scale(rng, shape, split, -0.22, 0.18) if split else 1.0
    result = jax.random.normal(rng, shape, jnp.float32) * spread * loudness
    return jnp.minimum(jnp.maximum(result, -bound), bound).astype(held_as)


def setup_inputs(seed: int = 0) -> dict:
    key_list = jax.random.split(jax.random.key(seed), 8)
    return {
        "tokens": bell_draw(key_list[0], (TOKENS, D), 1.0, 6.0, ((0, 8),)),
        "out_grad": bell_draw(key_list[1], (TOKENS, D), 1.0, 6.0, ((0, 8),)),
        "slot_params": bell_draw(key_list[2], (SLOT_ALL, D), 1.0, 6.0, ((0, 32),)),
        "first_mixing": bell_draw(key_list[3], (EXPERTS, N_PHM, N_PHM, N_PHM), 0.5, 3.0, ((0, 32),), jnp.float32),
        "first_blocks": bell_draw(key_list[4], (EXPERTS, N_PHM, DB, HBLOCK), D ** -0.5, 0.15625, ((0, 32), (3, 8))),
        "second_mixing": bell_draw(key_list[5], (EXPERTS, N_PHM, N_PHM, N_PHM), 0.5, 3.0, ((0, 32),), jnp.float32),
        "second_blocks": bell_draw(key_list[6], (EXPERTS, N_PHM, HBLOCK, DB), HID ** -0.5, 0.0625, ((0, 32), (2, 8))),
    }


logit_gain = 64.0
norm_eps = 1e-06
gelu_coef = 0.7978845608028654
cubic_coef = 0.044715

def gelu_pair(preact):
    inner_arg = gelu_coef * (preact + cubic_coef * preact * preact * preact)
    tangent = jnp.tanh(inner_arg)
    output = 0.5 * preact * (1.0 + tangent)
    slopes = 0.5 * (1.0 + tangent) + 0.5 * preact * (1.0 - tangent * tangent) * gelu_coef * (1.0 + 3.0 * cubic_coef * preact * preact)
    return (output, slopes)

def mix_blocks(blocks, mixing):
    return jnp.einsum('sak,iab->sbik', blocks.astype(jnp.float32), mixing.astype(jnp.float32))

def expert_grads(slot_in, grad_out, first_mixing, first_blocks, second_mixing, second_blocks):
    slots_here, model_width = slot_in.shape
    factors = first_mixing.shape[0]
    inner_width = model_width // factors
    hidden_block = first_blocks.shape[2]
    slot_split = slot_in.reshape(slots_here, factors, inner_width)
    first_flat = mix_blocks(slot_split, first_mixing).astype(jnp.bfloat16).reshape(slots_here * factors, factors * inner_width)
    first_matrix = first_blocks.reshape(factors * inner_width, hidden_block)
    preact = jnp.dot(first_flat, first_matrix, preferred_element_type=jnp.float32).reshape(slots_here, factors, hidden_block)
    activated, slopes = gelu_pair(preact)
    hidden = activated.astype(jnp.bfloat16)
    second_flat = mix_blocks(hidden, second_mixing).astype(jnp.bfloat16).reshape(slots_here * factors, factors * hidden_block)
    second_matrix = second_blocks.reshape(factors * hidden_block, inner_width)
    slot_out = jnp.dot(second_flat, second_matrix, preferred_element_type=jnp.float32).reshape(slots_here, model_width)
    grad_rows = grad_out.reshape(slots_here * factors, inner_width)
    grad_second_in = jnp.dot(grad_rows, second_matrix.T, preferred_element_type=jnp.float32).reshape(slots_here, factors, factors, hidden_block)
    grad_second_blocks = jnp.dot(second_flat.T, grad_rows, preferred_element_type=jnp.float32).reshape(factors, hidden_block, inner_width)
    grad_second_mixing = jnp.einsum('sak,sbik->iab', hidden.astype(jnp.float32), grad_second_in)
    grad_hidden = jnp.einsum('iab,sbik->sak', second_mixing.astype(jnp.float32), grad_second_in)
    grad_preact = (grad_hidden * slopes).astype(jnp.bfloat16).reshape(slots_here * factors, hidden_block)
    grad_first_in = jnp.dot(grad_preact, first_matrix.T, preferred_element_type=jnp.float32).reshape(slots_here, factors, factors, inner_width)
    grad_first_blocks = jnp.dot(first_flat.T, grad_preact, preferred_element_type=jnp.float32).reshape(factors, inner_width, hidden_block)
    grad_first_mixing = jnp.einsum('sad,sbid->iab', slot_split.astype(jnp.float32), grad_first_in)
    grad_slot = jnp.einsum('iab,sbid->sad', first_mixing.astype(jnp.float32), grad_first_in).reshape(slots_here, model_width)
    return (slot_out, grad_slot, grad_first_mixing, grad_first_blocks, grad_second_mixing, grad_second_blocks)

def reference(tokens, out_grad, slot_params, first_mixing, first_blocks, second_mixing, second_blocks):
    token_values = tokens.astype(jnp.float32)
    token_norm = jnp.sqrt(lax.optimization_barrier(jnp.sum(token_values * token_values, axis=1, keepdims=True)) + norm_eps)
    token_unit = token_values / token_norm
    token_unit_b = token_unit.astype(jnp.bfloat16)
    slot_values = slot_params.astype(jnp.float32)
    slot_norm = jnp.sqrt(lax.optimization_barrier(jnp.sum(slot_values * slot_values, axis=1, keepdims=True)) + norm_eps)
    slot_unit = slot_values / slot_norm
    slot_unit_b = slot_unit.astype(jnp.bfloat16)
    logits = logit_gain * jnp.dot(token_unit_b, slot_unit_b.T, preferred_element_type=jnp.float32)
    weights = jnp.exp(logits)
    dispatch_total = lax.optimization_barrier(jnp.sum(weights, axis=0))
    combine_total = lax.optimization_barrier(jnp.sum(weights, axis=1))
    slot_inputs = jnp.dot(weights.astype(jnp.bfloat16).T, tokens, preferred_element_type=jnp.float32) / dispatch_total[:, None]
    slot_inputs_b = slot_inputs.astype(jnp.bfloat16)
    dispatch = weights / dispatch_total[None, :]
    combine = weights / combine_total[:, None]
    slot_out_grad = jnp.dot(combine.astype(jnp.bfloat16).T, out_grad, preferred_element_type=jnp.float32).astype(jnp.bfloat16)
    results = jax.vmap(expert_grads)(slot_inputs_b.reshape(EXPERTS, SLOTS, D), slot_out_grad.reshape(EXPERTS, SLOTS, D), first_mixing, first_blocks, second_mixing, second_blocks)
    slot_out, slot_in_grad, grad_first_mixing, grad_first_blocks, grad_second_mixing, grad_second_blocks = results
    slot_out_b = slot_out.reshape(SLOT_ALL, D).astype(jnp.bfloat16)
    slot_in_grad = slot_in_grad.reshape(SLOT_ALL, D)
    slot_in_grad_b = slot_in_grad.astype(jnp.bfloat16)
    combine_grad = jnp.dot(out_grad, slot_out_b.T, preferred_element_type=jnp.float32)
    combine_dot = lax.optimization_barrier(jnp.sum(combine * combine_grad, axis=1))
    dispatch_grad = jnp.dot(tokens, slot_in_grad_b.T, preferred_element_type=jnp.float32)
    dispatch_dot = lax.optimization_barrier(jnp.sum(slot_inputs * slot_in_grad, axis=1))
    logit_grad = combine * (combine_grad - combine_dot[:, None]) + dispatch * (dispatch_grad - dispatch_dot[None, :])
    logit_grad_b = (logit_gain * logit_grad).astype(jnp.bfloat16)
    unit_grad_tokens = jnp.dot(logit_grad_b, slot_unit_b, preferred_element_type=jnp.float32)
    direct = jnp.dot(dispatch.astype(jnp.bfloat16), slot_in_grad_b, preferred_element_type=jnp.float32)
    grad_tokens = direct + (unit_grad_tokens - token_unit * lax.optimization_barrier(jnp.sum(token_unit * unit_grad_tokens, axis=1, keepdims=True))) / token_norm
    unit_grad_slots = jnp.dot(logit_grad_b.T, token_unit_b, preferred_element_type=jnp.float32)
    grad_slots = (unit_grad_slots - slot_unit * lax.optimization_barrier(jnp.sum(slot_unit * unit_grad_slots, axis=1, keepdims=True))) / slot_norm
    return (grad_tokens, grad_slots, grad_first_mixing, grad_first_blocks.astype(jnp.bfloat16), grad_second_mixing, grad_second_blocks.astype(jnp.bfloat16))
```

```python
import functools

import jax
import jax.numpy as jnp
from jax import lax
from jax.experimental import pallas as pl
from jax.experimental.pallas import tpu as pltpu
from jax.sharding import Mesh, PartitionSpec as P

logit_gain = 64.0
norm_eps = 1e-06
gelu_coef = 0.7978845608028654
cubic_coef = 0.044715

f32 = jnp.float32
bf16 = jnp.bfloat16
DIM = 1664
EXTRA = 128
DB = 416
NF = 4
ROWS = 16
HB = 256
TOK = 1024
CHUNK = 256
VMEM = pltpu.VMEM
SMEM = pltpu.SMEM
seq_axes = ("h", "x")
exp_axes = ("z", "y", "c")


def dot(a, b):
    return jnp.dot(a, b, preferred_element_type=f32)


def dot_t(a, b):
    return lax.dot_general(a, b, (((1,), (1,)), ((), ())), preferred_element_type=f32)


def dot_0(a, b):
    return lax.dot_general(a, b, (((0,), (0,)), ((), ())), preferred_element_type=f32)


def call(body, out, n_smem, n_in, flops, byts, name, scratch=()):
    return pl.pallas_call(
        body,
        out_shape=out,
        in_specs=[pl.BlockSpec(memory_space=SMEM)] * n_smem
        + [pl.BlockSpec(memory_space=VMEM)] * n_in,
        out_specs=jax.tree.map(lambda _: pl.BlockSpec(memory_space=VMEM), out),
        scratch_shapes=list(scratch),
        compiler_params=pltpu.CompilerParams(vmem_limit_bytes=32 << 20),
        cost_estimate=pl.CostEstimate(flops=flops, bytes_accessed=byts, transcendentals=0),
        name=name,
    )


def sds(shape, dtype):
    return jax.ShapeDtypeStruct(shape, dtype)


def unit_rows(values):
    norm = jnp.sqrt(jnp.sum(values * values, axis=1, keepdims=True) + norm_eps)
    return values / norm


def hi_lo(value, first):
    hi = value.astype(bf16).astype(f32)
    return jnp.where(first, hi, value - hi)


def split_blocks(rows):
    return jnp.concatenate([rows[:, a * DB : (a + 1) * DB] for a in range(NF)], axis=0)


def group(rows, a):
    return rows[a * ROWS : (a + 1) * ROWS]


def routing_body(tok_ref, slot_ref, w_ref, inv_ref, colsum_ref, pay_ref, acc_ref, tot_ref, col_ref):
    step = pl.program_id(0)
    tok = tok_ref[...]
    unit_b = unit_rows(slot_ref[...].astype(f32)).astype(bf16)
    inv = []
    for r in range(CHUNK // 128):
        part = tok_ref[pl.ds(r * 128, 128), :].astype(f32)
        sq = jnp.sum(part * part, axis=1, keepdims=True)
        inv.append(jnp.transpose(jnp.broadcast_to(sq, (128, 128)))[0:1])
    inv = lax.rsqrt(jnp.concatenate(inv, axis=1) + norm_eps)
    inv_ref[...] = inv
    w = jnp.exp(logit_gain * dot_t(unit_b, tok) * inv)
    w_ref[...] = w
    cols = jnp.sum(w, axis=0, keepdims=True)
    for r in range(CHUNK // 128):
        col_ref[pl.ds(step * (CHUNK // 128) + r, 1), :] = cols[:, r * 128 : (r + 1) * 128]
    part = dot(w.astype(bf16), tok)
    total = jnp.broadcast_to(jnp.sum(w, axis=1, keepdims=True), (w.shape[0], EXTRA))

    @pl.when(step == 0)
    def _():
        acc_ref[...] = part
        tot_ref[...] = total

    @pl.when(step > 0)
    def _():
        acc_ref[...] += part
        tot_ref[...] += total

    @pl.when(step == pl.num_programs(0) - 1)
    def _():
        lane = lax.broadcasted_iota(jnp.int32, tot_ref.shape, 1)
        pay_ref[:, :DIM] = acc_ref[...].astype(bf16)
        pay_ref[:, DIM:] = hi_lo(tot_ref[...], lane < 1).astype(bf16)
        colsum_ref[...] = jnp.broadcast_to(col_ref[...][None], colsum_ref.shape)


def routing(tokens, slot_params):
    slots = slot_params.shape[0]
    return pl.pallas_call(
        routing_body,
        grid=(TOK // CHUNK,),
        in_specs=[
            pl.BlockSpec((CHUNK, DIM), lambda i: (i, 0)),
            pl.BlockSpec((slots, DIM), lambda i: (0, 0)),
        ],
        out_specs=[
            pl.BlockSpec((slots, CHUNK), lambda i: (0, i)),
            pl.BlockSpec((1, CHUNK), lambda i: (0, i)),
            pl.BlockSpec((32, 8, 128), lambda i: (0, 0, 0)),
            pl.BlockSpec((slots, DIM + EXTRA), lambda i: (0, 0)),
        ],
        out_shape=[
            sds((slots, TOK), f32),
            sds((1, TOK), f32),
            sds((32, 8, 128), f32),
            sds((slots, DIM + EXTRA), bf16),
        ],
        scratch_shapes=[VMEM((slots, DIM), f32), VMEM((slots, EXTRA), f32), VMEM((8, 128), f32)],
        compiler_params=pltpu.CompilerParams(vmem_limit_bytes=32 << 20),
        cost_estimate=pl.CostEstimate(flops=4 * 32 * TOK * DIM, bytes_accessed=4 << 20, transcendentals=0),
        name="routing",
    )(tokens, slot_params)


def row_of(tile):
    return jnp.concatenate([tile[r : r + 1] for r in range(8)], axis=1)


def tile_of(row):
    return jnp.concatenate([row[:, r * 128 : (r + 1) * 128] for r in range(8)], axis=0)


def combine_body(parts_ref, w_ref, grad_ref, total_ref, out_ref):
    total = row_of(jnp.sum(parts_ref[...], axis=0))
    total_ref[...] = total
    combine = (w_ref[...] / total).astype(bf16)
    out_ref[...] = dot(combine, grad_ref[...]).astype(bf16)


def sum_parts(ref):
    total = ref[0].astype(f32)
    for k in range(1, ref.shape[0]):
        total = total + ref[k].astype(f32)
    return total


def forward_body(m1, m2, parts_ref, first_ref, second_ref, x_ref, xs_ref, dt_ref, y_ref, h_ref, sl_ref, s_ref, out_ref):
    total = sum_parts(parts_ref)
    dt = total[:, DIM : DIM + 1] + total[:, DIM + 1 : DIM + 2]
    dt_ref[...] = dt
    x = total[:, :DIM] / dt
    x_ref[...] = x
    xb = x.astype(bf16)
    for e in range(2):
        xs = split_blocks(xb[e * ROWS : (e + 1) * ROWS])
        xs_ref[e] = xs
        ys = [dot(xs, first_ref[e, i]) for i in range(NF)]
        for i in range(NF):
            y_ref[e, :, i * HB : (i + 1) * HB] = ys[i].astype(bf16)
        hid = []
        for b in range(NF):
            pre = None
            for i in range(NF):
                for a in range(NF):
                    term = m1[e, i * 16 + a * 4 + b] * group(ys[i], a)
                    pre = term if pre is None else pre + term
            inner = gelu_coef * (pre + cubic_coef * pre * pre * pre)
            tang = jnp.tanh(inner)
            hid_b = (0.5 * pre * (1.0 + tang)).astype(bf16)
            h_ref[e, b * ROWS : (b + 1) * ROWS, :] = hid_b
            hid.append(hid_b.astype(f32))
            sl_ref[e, b * ROWS : (b + 1) * ROWS, :] = 0.5 * (1.0 + tang) + 0.5 * pre * (
                1.0 - tang * tang
            ) * gelu_coef * (1.0 + 3.0 * cubic_coef * pre * pre)
        out = None
        for i in range(NF):
            rows = []
            for b in range(NF):
                acc = None
                for a in range(NF):
                    term = m2[e, i * 16 + a * 4 + b] * hid[a]
                    acc = term if acc is None else acc + term
                rows.append(acc.astype(bf16))
            si = jnp.concatenate(rows, axis=0)
            s_ref[e, :, i * HB : (i + 1) * HB] = si
            term = dot(si, second_ref[e, i])
            out = term if out is None else out + term
        for b in range(NF):
            out_ref[e * ROWS : (e + 1) * ROWS, b * DB : (b + 1) * DB] = group(out, b).astype(bf16)


def pair_sums(mats, same, column):
    rows = []
    for mat in mats:
        masked = jnp.where(same, mat, 0.0)
        for a in range(NF):
            rows.append(jnp.sum(group(masked, a), axis=0, keepdims=True))
    stack = jnp.concatenate(rows, axis=0)
    lane = lax.broadcasted_iota(jnp.int32, (NF * NF, EXTRA), 1)
    result = jnp.zeros((NF * NF, EXTRA), f32)
    for b in range(NF):
        value = jnp.sum(stack[:, b * ROWS : (b + 1) * ROWS], axis=1, keepdims=True)
        here = (lane == column + b) | (lane == column + b + 2 * NF)
        result = jnp.where(here, value, result)
    return result


def backward_body(m1, m2, parts_ref, first_ref, second_ref, y_ref, h_ref, sl_ref, gb_ref, hm_ref, out_ref):
    grad_b = sum_parts(parts_ref).astype(bf16)
    n = NF * ROWS
    r = lax.broadcasted_iota(jnp.int32, (n, n), 0)
    c = lax.broadcasted_iota(jnp.int32, (n, n), 1)
    same = (r & (ROWS - 1)) == (c & (ROWS - 1))
    lane = lax.broadcasted_iota(jnp.int32, (NF * NF, EXTRA), 1)
    for e in range(2):
        g = split_blocks(grad_b[e * ROWS : (e + 1) * ROWS])
        gb_ref[e] = g
        gs = [dot_t(g, second_ref[e, i]) for i in range(NF)]
        gps = []
        for a in range(NF):
            acc = None
            for i in range(NF):
                for b in range(NF):
                    term = m2[e, i * 16 + a * 4 + b] * group(gs[i], b)
                    acc = term if acc is None else acc + term
            gps.append((acc * sl_ref[e, a * ROWS : (a + 1) * ROWS, :]).astype(bf16))
        gp = jnp.concatenate(gps, axis=0)
        gpf = [v.astype(f32) for v in gps]
        out = None
        for i in range(NF):
            rows = []
            for a in range(NF):
                acc = None
                for b in range(NF):
                    term = m1[e, i * 16 + a * 4 + b] * gpf[b]
                    acc = term if acc is None else acc + term
                rows.append(acc.astype(bf16))
            hi = jnp.concatenate(rows, axis=0)
            hm_ref[e, :, i * HB : (i + 1) * HB] = hi
            term = dot_t(hi, first_ref[e, i])
            out = term if out is None else out + term
        for a in range(NF):
            out_ref[e * ROWS : (e + 1) * ROWS, a * DB : (a + 1) * DB] = group(out, a).astype(bf16)
        hid = h_ref[e]
        mix2 = pair_sums([dot_t(hid, gs[i].astype(bf16)) for i in range(NF)], same, NF)
        mix1 = pair_sums([dot_t(y_ref[e, :, i * HB : (i + 1) * HB], gp) for i in range(NF)], same, 0)
        out_ref[e * ROWS : (e + 1) * ROWS, DIM:] = hi_lo(mix1 + mix2, lane < 2 * NF).astype(bf16)


def weight_grad_body(xs_ref, hm_ref, s_ref, gb_ref, first_ref, second_ref):
    for e in range(2):
        for i in range(NF):
            cols = slice(i * HB, (i + 1) * HB)
            first_ref[e, i] = dot_0(xs_ref[e], hm_ref[e, :, cols]).astype(bf16)
            second_ref[e, i] = dot_0(s_ref[e, :, cols], gb_ref[e]).astype(bf16)


def combine_grad_body(parts_ref, grad_ref, w_ref, total_ref, cg_ref, cols_ref):
    out_b = sum_parts(parts_ref).astype(bf16)
    cg = dot_t(out_b, grad_ref[...])
    cg_ref[...] = cg
    combine = w_ref[...] / total_ref[...]
    cols = tile_of(jnp.sum(combine * cg, axis=0, keepdims=True))
    cols_ref[...] = jnp.broadcast_to(cols[None], cols_ref.shape)


def logit_body(parts_ref, x_ref, dt_ref, w_ref, total_ref, cg_ref, cdots_ref, inv_ref, tok_ref, pay_ref, ug_ref, mix_ref):
    total = sum_parts(parts_ref)
    mix_ref[...] = total[:, DIM:]
    grad = total[:, :DIM]
    grad_b = grad.astype(bf16)
    ddot = jnp.sum(x_ref[...] * grad, axis=1, keepdims=True)
    cdot = row_of(jnp.sum(cdots_ref[...], axis=0))
    tok = tok_ref[...]
    dg = dot_t(grad_b, tok)
    w = w_ref[...]
    combine = w / total_ref[...]
    dispatch = w / dt_ref[...]
    lg = combine * (cg_ref[...] - cdot) + dispatch * (dg - ddot)
    lgb = (logit_gain * lg * inv_ref[...]).astype(bf16)
    ug_ref[...] = dot(lgb, tok).astype(bf16)
    db = dispatch.astype(bf16)
    for k in range(4):
        pay_ref[k, :, :DIM] = grad_b
        pay_ref[k, :, DIM : DIM + 256] = lgb[:, k * 256 : (k + 1) * 256]
        pay_ref[k, :, DIM + 256 :] = db[:, k * 256 : (k + 1) * 256]


def token_body(core, recv_ref, slot_ref, tok_ref, keep_ref, send_ref):
    n = 4 * 32
    unit_b = unit_rows(slot_ref[...].reshape(n, DIM).astype(f32)).astype(bf16)
    recv = recv_ref[...].reshape(n, DIM + 512)
    grad = recv[:, :DIM]
    lgb = recv[:, DIM : DIM + 256]
    db = recv[:, DIM + 256 :]
    direct = dot_0(db, grad)
    through = dot_0(lgb, unit_b)
    first = core[0] == 0
    for y in range(4):
        pair = []
        for c in range(2):
            lo = (y * 2 + c) * 32
            t = tok_ref[lo : lo + 32, :].astype(f32)
            u = through[lo : lo + 32]
            n2 = jnp.sum(t * t, axis=1, keepdims=True) + norm_eps
            coef = jnp.sum(t * u, axis=1, keepdims=True) / n2
            pair.append(direct[lo : lo + 32] + u - t * coef)
        keep_ref[y] = jnp.where(first, pair[0], pair[1])
        send_ref[y] = jnp.where(first, pair[1], pair[0]).astype(bf16)


def slot_body(parts_ref, slot_ref, out_ref):
    ug = sum_parts(parts_ref)
    values = slot_ref[...].astype(f32)
    norm = jnp.sqrt(jnp.sum(values * values, axis=1, keepdims=True) + norm_eps)
    unit = values / norm
    out_ref[...] = (ug - unit * jnp.sum(unit * ug, axis=1, keepdims=True)) / norm


def swap(value, axis):
    return lax.ppermute(value, axis, [(0, 1), (1, 0)])


def spread(value, axes, count):
    return lax.all_to_all(jnp.broadcast_to(value[None], (count,) + value.shape), axes, 0, 0)


def seq_parts(value):
    both = (value.astype(f32) + swap(value, "h").astype(f32)).astype(bf16)
    return spread(both, "x", 4)


def local(tokens, out_grad, slot_params, first_mixing, first_blocks, second_mixing, second_blocks):
    m1 = first_mixing.reshape(2, NF * NF * NF)
    m2 = second_mixing.reshape(2, NF * NF * NF)
    slot_all = spread(slot_params, "z", 4)
    w, inv, colsum, input_part = routing(tokens, slot_params)
    col_parts = lax.all_to_all(colsum, exp_axes, 0, 0)
    input_parts = seq_parts(input_part)
    total, grad_part = call(
        combine_body, (sds((1, TOK), f32), sds((32, DIM), bf16)), 0, 3, 2 * 32 * TOK * DIM, 4 << 20, "combine"
    )(col_parts, w, out_grad)
    x, xs, dt, y, hid, slopes, second_in, out_part = call(
        forward_body,
        (
            sds((32, DIM), f32),
            sds((2, 64, DB), bf16),
            sds((32, 1), f32),
            sds((2, 64, NF * HB), bf16),
            sds((2, 64, HB), bf16),
            sds((2, 64, HB), f32),
            sds((2, 64, NF * HB), bf16),
            sds((32, DIM), bf16),
        ),
        2,
        3,
        4 * 128 * 1024 * DB,
        5 << 20,
        "forward",
    )(m1, m2, input_parts, first_blocks, second_blocks)
    grad_parts = seq_parts(grad_part)
    out_parts = seq_parts(out_part)
    gb, hm, input_grad_part = call(
        backward_body,
        (sds((2, 64, DB), bf16), sds((2, 64, NF * HB), bf16), sds((32, DIM + EXTRA), bf16)),
        2,
        6,
        4 * 128 * 1024 * DB,
        5 << 20,
        "backward",
    )(m1, m2, grad_parts, first_blocks, second_blocks, y, hid, slopes)
    input_grad_parts = seq_parts(input_grad_part)
    first_grad, second_grad = call(
        weight_grad_body,
        (sds(first_blocks.shape, bf16), sds(second_blocks.shape, bf16)),
        0,
        4,
        4 * 128 * 1024 * DB,
        5 << 20,
        "weight_grad",
    )(xs, hm, second_in, gb)
    cg, cols = call(
        combine_grad_body,
        (sds((32, TOK), f32), sds((32, 8, 128), f32)),
        0,
        4,
        2 * 32 * TOK * DIM,
        4 << 20,
        "combine_grad",
    )(out_parts, out_grad, w, total)
    cdots = lax.all_to_all(cols, exp_axes, 0, 0)
    pay, ug_part, mix = call(
        logit_body,
        (sds((4, 32, DIM + 512), bf16), sds((32, DIM), bf16), sds((32, EXTRA), f32)),
        0,
        9,
        4 * 32 * TOK * DIM,
        4 << 20,
        "logit_grad",
    )(input_grad_parts, x, dt, w, total, cg, cdots, inv, tokens)
    recv = lax.all_to_all(pay, "z", 0, 0)
    ug_parts = seq_parts(ug_part)
    quarter = lax.dynamic_slice_in_dim(tokens, lax.axis_index("z") * 256, 256, 0)
    core = lax.axis_index("c").astype(jnp.int32).reshape(1)
    keep, send = call(
        token_body,
        (sds((4, 32, DIM), f32), sds((4, 32, DIM), bf16)),
        1,
        3,
        4 * 128 * 256 * DIM,
        4 << 20,
        "token_grad",
    )(core, recv, slot_all, quarter)
    half = (keep + swap(send, "c").astype(f32)).astype(bf16)
    grad_tokens = jnp.sum(lax.all_to_all(half, "y", 0, 0).astype(f32), axis=0)
    grad_slots = call(
        slot_body, sds((32, DIM), f32), 0, 2, 32 * DIM * 8, 1 << 20, "slot_grad"
    )(ug_parts, slot_params)
    mixes = (mix[:, : 2 * NF] + mix[:, 2 * NF : 4 * NF]).reshape(2, NF, NF, 2, NF)
    return (
        grad_tokens,
        grad_slots,
        mixes[:, :, :, 0],
        first_grad,
        mixes[:, :, :, 1],
        second_grad,
    )


def solution(mesh):
    fine = Mesh(mesh.devices.reshape(2, 4, 4, 4, 2), seq_axes + exp_axes)
    return jax.shard_map(
        local,
        mesh=fine,
        in_specs=(
            P(seq_axes, None),
            P(seq_axes, None),
            P(exp_axes, None),
            P(exp_axes, None, None, None),
            P(exp_axes, None, None, seq_axes),
            P(exp_axes, None, None, None),
            P(exp_axes, None, seq_axes, None),
        ),
        out_specs=(
            P(seq_axes + exp_axes, None),
            P(exp_axes, None),
            P(exp_axes, None, None, None),
            P(exp_axes, None, None, seq_axes),
            P(exp_axes, None, None, None),
            P(exp_axes, None, seq_axes, None),
        ),
        check_vma=False,
    )
```

```python
import jax
import jax.numpy as jnp
from jax import lax
from jax.experimental import pallas as pl
from jax.experimental.pallas import tpu as pltpu
from jax.sharding import Mesh, PartitionSpec as P

logit_gain = 64.0
norm_eps = 1e-06
gelu_coef = 0.7978845608028654
cubic_coef = 0.044715

f32 = jnp.float32
bf16 = jnp.bfloat16
DIM = 1664
EXTRA = 128
DB = 416
NF = 4
ROWS = 16
HB = 256
TOK = 1024
CHUNK = 256
STEPS = TOK // CHUNK
WIDE = 60 << 20
SMALL = 52 << 20
SIDE = 2 * NF * HB
VMEM = pltpu.VMEM
SMEM = pltpu.SMEM
seq_axes = ("h", "x")
exp_axes = ("z", "y", "c")


def dot(a, b):
    return jnp.dot(a, b, preferred_element_type=f32)


def dot_t(a, b):
    return lax.dot_general(a, b, (((1,), (1,)), ((), ())), preferred_element_type=f32)


def dot_0(a, b):
    return lax.dot_general(a, b, (((0,), (0,)), ((), ())), preferred_element_type=f32)


def call(body, out, n_smem, args, flops, byts, name, streamed=False):
    ins = [pl.BlockSpec(memory_space=VMEM)] * (len(args) - n_smem)
    scratch = []
    if streamed:
        ins[-1] = pl.BlockSpec(memory_space=pl.ANY)
        scratch = [VMEM(args[-1].shape, args[-1].dtype), pltpu.SemaphoreType.DMA((STEPS,))]
    return pl.pallas_call(
        body,
        out_shape=out,
        in_specs=[pl.BlockSpec(memory_space=SMEM)] * n_smem + ins,
        out_specs=jax.tree.map(lambda o: pl.BlockSpec(memory_space=VMEM), out),
        scratch_shapes=scratch,
        compiler_params=pltpu.CompilerParams(vmem_limit_bytes=WIDE if streamed else SMALL),
        cost_estimate=pl.CostEstimate(flops=flops, bytes_accessed=byts, transcendentals=0),
        name=name,
    )(*args)


def stream(source, target, sems):
    copies = []
    for k in range(STEPS):
        rows = pl.ds(k * CHUNK, CHUNK)
        copies.append(pltpu.make_async_copy(source.at[rows], target.at[rows], sems.at[k]))
        copies[-1].start()
    return copies


def chunk(k):
    return slice(k * CHUNK, (k + 1) * CHUNK)


def sds(shape, dtype):
    return jax.ShapeDtypeStruct(shape, dtype)


def unit_rows(values):
    norm = jnp.sqrt(jnp.sum(values * values, axis=1, keepdims=True) + norm_eps)
    return values / norm


def hi_lo(value, first):
    hi = value.astype(bf16).astype(f32)
    return jnp.where(first, hi, value - hi)


def split_blocks(rows):
    return jnp.concatenate([rows[:, a * DB : (a + 1) * DB] for a in range(NF)], axis=0)


def group(rows, a):
    return rows[a * ROWS : (a + 1) * ROWS]


def routing_body(slot_ref, tok_hbm, w_ref, colsum_ref, pay_ref, tok_ref, sems):
    copies = stream(tok_hbm, tok_ref, sems)
    unit_b = unit_rows(slot_ref[...].astype(f32)).astype(bf16)
    acc = jnp.zeros(slot_ref.shape, f32)
    total = jnp.zeros((slot_ref.shape[0], 1), f32)
    tiles = []
    for k in range(STEPS):
        copies[k].wait()
        inv = []
        for r in range(CHUNK // 128):
            part = tok_ref[k * CHUNK + r * 128 : k * CHUNK + (r + 1) * 128, :].astype(f32)
            sq = jnp.sum(part * part, axis=1, keepdims=True)
            inv.append(jnp.transpose(jnp.broadcast_to(sq, (128, 128)))[0:1])
        inv = lax.rsqrt(jnp.concatenate(inv, axis=1) + norm_eps)
        cols = chunk(k)
        w_ref[32:, cols] = jnp.broadcast_to(inv, (8, CHUNK))
        tok = tok_ref[cols, :]
        w = jnp.exp(logit_gain * dot_t(unit_b, tok) * inv)
        w_ref[:32, cols] = w
        sums = jnp.sum(w, axis=0, keepdims=True)
        tiles += [sums[:, r * 128 : (r + 1) * 128] for r in range(CHUNK // 128)]
        acc = acc + dot(w.astype(bf16), tok)
        total = total + jnp.sum(w, axis=1, keepdims=True)
    wide = jnp.broadcast_to(total, (total.shape[0], EXTRA))
    lane = lax.broadcasted_iota(jnp.int32, wide.shape, 1)
    pay_ref[:, :DIM] = acc.astype(bf16)
    pay_ref[:, DIM:] = hi_lo(wide, lane < 1).astype(bf16)
    cols = jnp.concatenate(tiles, axis=0)
    colsum_ref[...] = jnp.broadcast_to(cols[None], colsum_ref.shape)


def row_of(tile):
    return jnp.concatenate([tile[r : r + 1] for r in range(8)], axis=1)


def tile_of(row):
    return jnp.concatenate([row[:, r * 128 : (r + 1) * 128] for r in range(8)], axis=0)


def combine_body(parts_ref, w_ref, grad_ref, total_ref, out_ref):
    total = row_of(jnp.sum(parts_ref[...], axis=0))
    total_ref[...] = total
    combine = (w_ref[:32] / total).astype(bf16)
    out_ref[...] = dot(combine, grad_ref[...]).astype(bf16)


def sum_parts(ref):
    total = ref[0].astype(f32)
    for k in range(1, ref.shape[0]):
        total = total + ref[k].astype(f32)
    return total


def sum_ring(a, b, c, d):
    return (a[...].astype(f32) + c[...].astype(f32)) + (b[...].astype(f32) + d[...].astype(f32))


def forward_body(m1, m2, p0, p1, p2, p3, first_ref, second_ref, x_ref, side_ref, sl_ref, out_ref):
    total = sum_ring(p0, p1, p2, p3)
    dt = total[:, DIM : DIM + 1] + total[:, DIM + 1 : DIM + 2]
    x_ref[:, DIM:] = jnp.broadcast_to(dt, (dt.shape[0], EXTRA))
    x = total[:, :DIM] / dt
    x_ref[:, :DIM] = x
    xb = x.astype(bf16)
    for e in range(2):
        xs = split_blocks(xb[e * ROWS : (e + 1) * ROWS])
        ys = [dot(xs, first_ref[e, i]) for i in range(NF)]
        for i in range(NF):
            side_ref[e, :, i * HB : (i + 1) * HB] = ys[i].astype(bf16)
        hid = []
        for b in range(NF):
            pre = None
            for i in range(NF):
                for a in range(NF):
                    term = m1[e, i, a, b] * group(ys[i], a)
                    pre = term if pre is None else pre + term
            inner = gelu_coef * (pre + cubic_coef * pre * pre * pre)
            tang = jnp.tanh(inner)
            hid_b = (0.5 * pre * (1.0 + tang)).astype(bf16)
            side_ref[e, b * ROWS : (b + 1) * ROWS, SIDE:] = hid_b
            hid.append(hid_b.astype(f32))
            sl_ref[e, b * ROWS : (b + 1) * ROWS, :] = 0.5 * (1.0 + tang) + 0.5 * pre * (
                1.0 - tang * tang
            ) * gelu_coef * (1.0 + 3.0 * cubic_coef * pre * pre)
        out = None
        for i in range(NF):
            rows = []
            for b in range(NF):
                acc = None
                for a in range(NF):
                    term = m2[e, i, a, b] * hid[a]
                    acc = term if acc is None else acc + term
                rows.append(acc.astype(bf16))
            si = jnp.concatenate(rows, axis=0)
            side_ref[e, :, (NF + i) * HB : (NF + i + 1) * HB] = si
            term = dot_t(si, second_ref[e, i])
            out = term if out is None else out + term
        for b in range(NF):
            out_ref[e * ROWS : (e + 1) * ROWS, b * DB : (b + 1) * DB] = group(out, b).astype(bf16)


def pair_sums(mats, same, column):
    rows = []
    for mat in mats:
        masked = jnp.where(same, mat, 0.0)
        for a in range(NF):
            rows.append(jnp.sum(group(masked, a), axis=0, keepdims=True))
    stack = jnp.concatenate(rows, axis=0)
    lane = lax.broadcasted_iota(jnp.int32, (NF * NF, EXTRA), 1)
    result = jnp.zeros((NF * NF, EXTRA), f32)
    for b in range(NF):
        value = jnp.sum(stack[:, b * ROWS : (b + 1) * ROWS], axis=1, keepdims=True)
        here = (lane == column + b) | (lane == column + b + 2 * NF)
        result = jnp.where(here, value, result)
    return result


def backward_body(m1, m2, parts_ref, first_ref, second_ref, side_ref, sl_ref, hg_ref, out_ref):
    grad_b = sum_parts(parts_ref).astype(bf16)
    n = NF * ROWS
    r = lax.broadcasted_iota(jnp.int32, (n, n), 0)
    c = lax.broadcasted_iota(jnp.int32, (n, n), 1)
    same = (r & (ROWS - 1)) == (c & (ROWS - 1))
    lane = lax.broadcasted_iota(jnp.int32, (NF * NF, EXTRA), 1)
    for e in range(2):
        g = split_blocks(grad_b[e * ROWS : (e + 1) * ROWS])
        hg_ref[e, :, NF * HB : NF * HB + DB] = g
        gs = [dot(g, second_ref[e, i]) for i in range(NF)]
        gps = []
        for a in range(NF):
            acc = None
            for i in range(NF):
                for b in range(NF):
                    term = m2[e, i, a, b] * group(gs[i], b)
                    acc = term if acc is None else acc + term
            gps.append((acc * sl_ref[e, a * ROWS : (a + 1) * ROWS, :]).astype(bf16))
        gp = jnp.concatenate(gps, axis=0)
        gpf = [v.astype(f32) for v in gps]
        out = None
        for i in range(NF):
            rows = []
            for a in range(NF):
                acc = None
                for b in range(NF):
                    term = m1[e, i, a, b] * gpf[b]
                    acc = term if acc is None else acc + term
                rows.append(acc.astype(bf16))
            hi = jnp.concatenate(rows, axis=0)
            hg_ref[e, :, i * HB : (i + 1) * HB] = hi
            term = dot_t(hi, first_ref[e, i])
            out = term if out is None else out + term
        for a in range(NF):
            out_ref[e * ROWS : (e + 1) * ROWS, a * DB : (a + 1) * DB] = group(out, a).astype(bf16)
        hid = side_ref[e, :, SIDE:]
        mix2 = pair_sums([dot_t(hid, gs[i].astype(bf16)) for i in range(NF)], same, NF)
        mix1 = pair_sums([dot_t(side_ref[e, :, i * HB : (i + 1) * HB], gp) for i in range(NF)], same, 0)
        out_ref[e * ROWS : (e + 1) * ROWS, DIM:] = hi_lo(mix1 + mix2, lane < 2 * NF).astype(bf16)


def weight_grad_body(x_ref, side_ref, hg_ref, first_ref, second_ref):
    for e in range(2):
        xs = split_blocks(x_ref[e * ROWS : (e + 1) * ROWS, :DIM].astype(bf16))
        g = hg_ref[e, :, NF * HB : NF * HB + DB]
        for i in range(NF):
            first_ref[e, i] = dot_0(xs, hg_ref[e, :, i * HB : (i + 1) * HB]).astype(bf16)
            second_ref[e, i] = dot_0(g, side_ref[e, :, (NF + i) * HB : (NF + i + 1) * HB]).astype(bf16)


def combine_grad_body(parts_ref, w_ref, total_ref, grad_ref, cg_ref, cols_ref):
    out_b = sum_parts(parts_ref).astype(bf16)
    cg = dot_t(out_b, grad_ref[...])
    total = total_ref[...]
    cg_ref[:32] = cg
    cg_ref[32:] = jnp.broadcast_to(total, (8, TOK))
    cols = tile_of(jnp.sum(w_ref[:32] / total * cg, axis=0, keepdims=True))
    cols_ref[...] = jnp.broadcast_to(cols[None], cols_ref.shape)


def logit_body(p0, p1, p2, p3, cdots_ref, x_ref, w_ref, cg_ref, tok_ref, pay_ref, ug_ref, mix_ref):
    total = sum_ring(p0, p1, p2, p3)
    mix_ref[...] = total[:, DIM:]
    grad = total[:, :DIM]
    grad_b = grad.astype(bf16)
    ddot = jnp.sum(x_ref[:, :DIM] * grad, axis=1, keepdims=True)
    cdot = row_of(jnp.sum(cdots_ref[...], axis=0))
    tok = tok_ref[...]
    dg = dot_t(grad_b, tok)
    w = w_ref[:32]
    combine = w / cg_ref[32:33]
    dispatch = w / x_ref[:, DIM : DIM + 1]
    lg = combine * (cg_ref[:32] - cdot) + dispatch * (dg - ddot)
    lgb = (logit_gain * lg * w_ref[32:33]).astype(bf16)
    ug_ref[...] = dot(lgb, tok).astype(bf16)
    db = dispatch.astype(bf16)
    for k in range(STEPS):
        pay_ref[k, :, :DIM] = grad_b
        pay_ref[k, :, DIM : DIM + CHUNK] = lgb[:, chunk(k)]
        pay_ref[k, :, DIM + CHUNK :] = db[:, chunk(k)]


def token_body(place, recv_ref, s0, s1, s2, s3, tok_ref, keep_ref, send_ref):
    direct = None
    through = None
    for k, slot_ref in enumerate((s0, s1, s2, s3)):
        at = (place[0] + 4 - k) & 3
        unit_b = unit_rows(slot_ref[...].astype(f32)).astype(bf16)
        d = dot_0(recv_ref[at, :, DIM + CHUNK :], recv_ref[at, :, :DIM])
        u = dot_0(recv_ref[at, :, DIM : DIM + CHUNK], unit_b)
        direct = d if direct is None else direct + d
        through = u if through is None else through + u
    first = place[1] == 0
    for y in range(4):
        pair = []
        for c in range(2):
            lo = (y * 2 + c) * 32
            t = tok_ref[lo : lo + 32, :].astype(f32)
            u = through[lo : lo + 32]
            n2 = jnp.sum(t * t, axis=1, keepdims=True) + norm_eps
            coef = jnp.sum(t * u, axis=1, keepdims=True) / n2
            pair.append(direct[lo : lo + 32] + u - t * coef)
        keep_ref[y] = jnp.where(first, pair[0], pair[1])
        send_ref[y] = jnp.where(first, pair[1], pair[0]).astype(bf16)


def slot_body(p0, p1, p2, p3, slot_ref, out_ref):
    ug = sum_ring(p0, p1, p2, p3)
    values = slot_ref[...].astype(f32)
    norm = jnp.sqrt(jnp.sum(values * values, axis=1, keepdims=True) + norm_eps)
    unit = values / norm
    out_ref[...] = (ug - unit * jnp.sum(unit * ug, axis=1, keepdims=True)) / norm


def swap(value, axis):
    return lax.ppermute(value, axis, [(0, 1), (1, 0)])


def exchange(value, axes):
    return lax.all_to_all(value, axes, 0, 0)


def ring(value, axis):
    pairs = [[(i, (i + k) % 4) for i in range(4)] for k in range(1, 4)]
    return [value] + [lax.ppermute(value, axis, p) for p in pairs]


def far_sum(value):
    return (value.astype(f32) + swap(value, "h").astype(f32)).astype(bf16)


def gather_x(value):
    return exchange(jnp.broadcast_to(value[None], (4,) + value.shape), "x")


tie = lax.optimization_barrier


def local(tokens, out_grad, slot_params, m1, first_blocks, m2, second_blocks):
    second_turned = jnp.swapaxes(second_blocks, 2, 3)
    slot_all = ring(slot_params, "z")
    w, colsum, input_part = call(
        routing_body,
        (sds((40, TOK), f32), sds((32, 8, 128), f32), sds((32, DIM + EXTRA), bf16)),
        0,
        (slot_params, tokens),
        4 * 32 * TOK * DIM,
        4 << 20,
        "routing",
        True,
    )
    input_far = far_sum(input_part)
    col_parts = exchange(colsum, exp_axes)
    col_parts, input_far, *slot_all = tie((col_parts, input_far, *slot_all))
    total, grad_part = call(
        combine_body,
        (sds((1, TOK), f32), sds((32, DIM), bf16)),
        0,
        (col_parts, w, out_grad),
        2 * 32 * TOK * DIM,
        4 << 20,
        "combine",
    )
    input_parts = ring(input_far, "x")
    grad_far = far_sum(grad_part)
    *input_parts, grad_far = tie((*input_parts, grad_far))
    grad_parts = gather_x(grad_far)
    x, side, slopes, out_part = call(
        forward_body,
        (
            sds((32, DIM + EXTRA), f32),
            sds((2, 64, SIDE + HB), bf16),
            sds((2, 64, HB), f32),
            sds((32, DIM), bf16),
        ),
        2,
        (m1, m2, *input_parts, first_blocks, second_turned),
        4 * 128 * 1024 * DB,
        5 << 20,
        "forward",
    )
    out_far = far_sum(out_part)
    hg, input_grad_part = call(
        backward_body,
        (sds((2, 64, NF * HB + 512), bf16), sds((32, DIM + EXTRA), bf16)),
        2,
        (m1, m2, grad_parts, first_blocks, second_turned, side, slopes),
        4 * 128 * 1024 * DB,
        5 << 20,
        "backward",
    )
    out_parts = gather_x(out_far)
    input_grad_far = far_sum(input_grad_part)
    out_parts, input_grad_far = tie((out_parts, input_grad_far))
    input_grad_parts = ring(input_grad_far, "x")
    cg, cols = call(
        combine_grad_body,
        (sds((40, TOK), f32), sds((32, 8, 128), f32)),
        0,
        (out_parts, w, total, out_grad),
        2 * 32 * TOK * DIM,
        4 << 20,
        "combine_grad",
    )
    cdots = exchange(cols, exp_axes)
    pay, ug_part, mix = call(
        logit_body,
        (sds((4, 32, DIM + 512), bf16), sds((32, DIM), bf16), sds((32, EXTRA), f32)),
        0,
        (*input_grad_parts, cdots, x, w, cg, tokens),
        4 * 32 * TOK * DIM,
        4 << 20,
        "logit_grad",
    )
    first_grad, second_grad = call(
        weight_grad_body,
        (sds(first_blocks.shape, bf16), sds(second_turned.shape, bf16)),
        0,
        (x, side, hg),
        4 * 128 * 1024 * DB,
        5 << 20,
        "weight_grad",
    )
    recv = exchange(pay, "z")
    ug_far = far_sum(ug_part)
    recv, ug_far = tie((recv, ug_far))
    ug_parts = ring(ug_far, "x")
    quarter = lax.dynamic_slice_in_dim(tokens, lax.axis_index("z") * 256, 256, 0)
    place = jnp.stack([lax.axis_index("z"), lax.axis_index("c")]).astype(jnp.int32)
    keep, send = call(
        token_body,
        (sds((4, 32, DIM), f32), sds((4, 32, DIM), bf16)),
        1,
        (place, recv, *slot_all, quarter),
        4 * 128 * 256 * DIM,
        4 << 20,
        "token_grad",
    )
    half = (keep + swap(send, "c").astype(f32)).astype(bf16)
    grad_tokens = jnp.sum(exchange(half, "y").astype(f32), axis=0)
    grad_slots = call(
        slot_body, sds((32, DIM), f32), 0, (*ug_parts, slot_params), 32 * DIM * 8, 1 << 20, "slot_grad"
    )
    mixes = (mix[:, : 2 * NF] + mix[:, 2 * NF : 4 * NF]).reshape(2, NF, NF, 2, NF)
    return (
        grad_tokens,
        grad_slots,
        mixes[:, :, :, 0],
        first_grad,
        mixes[:, :, :, 1],
        jnp.swapaxes(second_grad, 2, 3),
    )


def solution(mesh):
    fine = Mesh(mesh.devices.reshape(2, 4, 4, 4, 2), seq_axes + exp_axes)
    return jax.shard_map(
        local,
        mesh=fine,
        in_specs=(
            P(seq_axes, None),
            P(seq_axes, None),
            P(exp_axes, None),
            P(exp_axes, None, None, None),
            P(exp_axes, None, None, seq_axes),
            P(exp_axes, None, None, None),
            P(exp_axes, None, seq_axes, None),
        ),
        out_specs=(
            P(seq_axes + exp_axes, None),
            P(exp_axes, None),
            P(exp_axes, None, None, None),
            P(exp_axes, None, None, seq_axes),
            P(exp_axes, None, None, None),
            P(exp_axes, None, seq_axes, None),
        ),
        check_vma=False,
    )
```

```python
import jax
import jax.numpy as jnp
from jax import lax
from jax.experimental import pallas as pl
from jax.experimental.pallas import tpu as pltpu
from jax.sharding import Mesh, PartitionSpec as P

logit_gain = 64.0
norm_eps = 1e-06
gelu_coef = 0.7978845608028654
cubic_coef = 0.044715

f32 = jnp.float32
bf16 = jnp.bfloat16
DIM = 1664
EXTRA = 128
DB = 416
NF = 4
ROWS = 16
HB = 256
TOK = 1024
CHUNK = 256
STEPS = TOK // CHUNK
WIDE = 60 << 20
SMALL = 51 << 20
SIDE = 2 * NF * HB
VMEM = pltpu.VMEM
SMEM = pltpu.SMEM
seq_axes = ("h", "x")
exp_axes = ("z", "y", "c")


def dot(a, b):
    return jnp.dot(a, b, preferred_element_type=f32)


def dot_t(a, b):
    return lax.dot_general(a, b, (((1,), (1,)), ((), ())), preferred_element_type=f32)


def dot_0(a, b):
    return lax.dot_general(a, b, (((0,), (0,)), ((), ())), preferred_element_type=f32)


def call(body, out, n_smem, args, flops, byts, name, streamed=False):
    ins = [pl.BlockSpec(memory_space=VMEM)] * (len(args) - n_smem)
    scratch = []
    if streamed:
        ins[-1] = pl.BlockSpec(memory_space=pl.ANY)
        scratch = [VMEM(args[-1].shape, args[-1].dtype), pltpu.SemaphoreType.DMA((STEPS,))]
    return pl.pallas_call(
        body,
        out_shape=out,
        in_specs=[pl.BlockSpec(memory_space=SMEM)] * n_smem + ins,
        out_specs=jax.tree.map(lambda o: pl.BlockSpec(memory_space=VMEM), out),
        scratch_shapes=scratch,
        compiler_params=pltpu.CompilerParams(vmem_limit_bytes=WIDE if streamed else SMALL),
        cost_estimate=pl.CostEstimate(flops=flops, bytes_accessed=byts, transcendentals=0),
        name=name,
    )(*args)


def stream(source, target, sems):
    copies = []
    for k in range(STEPS):
        rows = pl.ds(k * CHUNK, CHUNK)
        copies.append(pltpu.make_async_copy(source.at[rows], target.at[rows], sems.at[k]))
        copies[-1].start()
    return copies


def chunk(k):
    return slice(k * CHUNK, (k + 1) * CHUNK)


def sds(shape, dtype):
    return jax.ShapeDtypeStruct(shape, dtype)


def unit_rows(values):
    norm = jnp.sqrt(jnp.sum(values * values, axis=1, keepdims=True) + norm_eps)
    return values / norm


def hi_lo(value, first):
    hi = value.astype(bf16).astype(f32)
    return jnp.where(first, hi, value - hi)


def split_blocks(rows):
    return jnp.concatenate([rows[:, a * DB : (a + 1) * DB] for a in range(NF)], axis=0)


def group(rows, a):
    return rows[a * ROWS : (a + 1) * ROWS]


def routing_body(slot_ref, tok_hbm, w_ref, colsum_ref, pay_ref, tok_ref, sems):
    copies = stream(tok_hbm, tok_ref, sems)
    unit_b = unit_rows(slot_ref[...].astype(f32)).astype(bf16)
    acc = jnp.zeros(slot_ref.shape, f32)
    total = jnp.zeros((slot_ref.shape[0], 1), f32)
    tiles = []
    for k in range(STEPS):
        copies[k].wait()
        inv = []
        for r in range(CHUNK // 128):
            part = tok_ref[k * CHUNK + r * 128 : k * CHUNK + (r + 1) * 128, :].astype(f32)
            sq = jnp.sum(part * part, axis=1, keepdims=True)
            inv.append(jnp.transpose(jnp.broadcast_to(sq, (128, 128)))[0:1])
        inv = lax.rsqrt(jnp.concatenate(inv, axis=1) + norm_eps)
        cols = chunk(k)
        w_ref[32:, cols] = jnp.broadcast_to(inv, (8, CHUNK))
        tok = tok_ref[cols, :]
        w = jnp.exp(logit_gain * dot_t(unit_b, tok) * inv)
        w_ref[:32, cols] = w
        sums = jnp.sum(w, axis=0, keepdims=True)
        tiles += [sums[:, r * 128 : (r + 1) * 128] for r in range(CHUNK // 128)]
        acc = acc + dot(w.astype(bf16), tok)
        total = total + jnp.sum(w, axis=1, keepdims=True)
    wide = jnp.broadcast_to(total, (total.shape[0], EXTRA))
    lane = lax.broadcasted_iota(jnp.int32, wide.shape, 1)
    pay_ref[:, :DIM] = acc.astype(bf16)
    pay_ref[:, DIM:] = hi_lo(wide, lane < 1).astype(bf16)
    cols = jnp.concatenate(tiles, axis=0)
    colsum_ref[...] = jnp.broadcast_to(cols[None], colsum_ref.shape)


def row_of(tile):
    return jnp.concatenate([tile[r : r + 1] for r in range(8)], axis=1)


def tile_of(row):
    return jnp.concatenate([row[:, r * 128 : (r + 1) * 128] for r in range(8)], axis=0)


def combine_body(parts_ref, w_ref, grad_ref, total_ref, out_ref):
    total = row_of(jnp.sum(parts_ref[...], axis=0))
    total_ref[...] = total
    combine = (w_ref[:32] / total).astype(bf16)
    out_ref[...] = dot(combine, grad_ref[...]).astype(bf16)


def sum_parts(ref):
    total = ref[0].astype(f32)
    for k in range(1, ref.shape[0]):
        total = total + ref[k].astype(f32)
    return total


def sum_ring(a, b, c, d):
    return (a[...].astype(f32) + c[...].astype(f32)) + (b[...].astype(f32) + d[...].astype(f32))


def forward_body(m1, m2, p0, p1, p2, p3, first_ref, second_ref, x_ref, side_ref, sl_ref, out_ref):
    total = sum_ring(p0, p1, p2, p3)
    dt = total[:, DIM : DIM + 1] + total[:, DIM + 1 : DIM + 2]
    x_ref[:, DIM:] = jnp.broadcast_to(dt, (dt.shape[0], EXTRA))
    x = total[:, :DIM] / dt
    x_ref[:, :DIM] = x
    xb = x.astype(bf16)
    for e in range(2):
        xs = split_blocks(xb[e * ROWS : (e + 1) * ROWS])
        ys = [dot(xs, first_ref[e, i]) for i in range(NF)]
        for i in range(NF):
            side_ref[e, :, i * HB : (i + 1) * HB] = ys[i].astype(bf16)
        hid = []
        for b in range(NF):
            pre = None
            for i in range(NF):
                for a in range(NF):
                    term = m1[e, i, a, b] * group(ys[i], a)
                    pre = term if pre is None else pre + term
            inner = gelu_coef * (pre + cubic_coef * pre * pre * pre)
            tang = jnp.tanh(inner)
            hid_b = (0.5 * pre * (1.0 + tang)).astype(bf16)
            side_ref[e, b * ROWS : (b + 1) * ROWS, SIDE:] = hid_b
            hid.append(hid_b.astype(f32))
            sl_ref[e, b * ROWS : (b + 1) * ROWS, :] = 0.5 * (1.0 + tang) + 0.5 * pre * (
                1.0 - tang * tang
            ) * gelu_coef * (1.0 + 3.0 * cubic_coef * pre * pre)
        out = None
        for i in range(NF):
            rows = []
            for b in range(NF):
                acc = None
                for a in range(NF):
                    term = m2[e, i, a, b] * hid[a]
                    acc = term if acc is None else acc + term
                rows.append(acc.astype(bf16))
            si = jnp.concatenate(rows, axis=0)
            side_ref[e, :, (NF + i) * HB : (NF + i + 1) * HB] = si
            term = dot_t(si, second_ref[e, i])
            out = term if out is None else out + term
        for b in range(NF):
            out_ref[e * ROWS : (e + 1) * ROWS, b * DB : (b + 1) * DB] = group(out, b).astype(bf16)


def pair_sums(mats, same, column):
    rows = []
    for mat in mats:
        masked = jnp.where(same, mat, 0.0)
        for a in range(NF):
            rows.append(jnp.sum(group(masked, a), axis=0, keepdims=True))
    stack = jnp.concatenate(rows, axis=0)
    lane = lax.broadcasted_iota(jnp.int32, (NF * NF, EXTRA), 1)
    result = jnp.zeros((NF * NF, EXTRA), f32)
    for b in range(NF):
        value = jnp.sum(stack[:, b * ROWS : (b + 1) * ROWS], axis=1, keepdims=True)
        here = (lane == column + b) | (lane == column + b + 2 * NF)
        result = jnp.where(here, value, result)
    return result


def backward_body(m1, m2, parts_ref, first_ref, second_ref, side_ref, sl_ref, hg_ref, out_ref):
    grad_b = sum_parts(parts_ref).astype(bf16)
    n = NF * ROWS
    r = lax.broadcasted_iota(jnp.int32, (n, n), 0)
    c = lax.broadcasted_iota(jnp.int32, (n, n), 1)
    same = (r & (ROWS - 1)) == (c & (ROWS - 1))
    lane = lax.broadcasted_iota(jnp.int32, (NF * NF, EXTRA), 1)
    for e in range(2):
        g = split_blocks(grad_b[e * ROWS : (e + 1) * ROWS])
        hg_ref[e, :, NF * HB : NF * HB + DB] = g
        gs = [dot(g, second_ref[e, i]) for i in range(NF)]
        gps = []
        for a in range(NF):
            acc = None
            for i in range(NF):
                for b in range(NF):
                    term = m2[e, i, a, b] * group(gs[i], b)
                    acc = term if acc is None else acc + term
            gps.append((acc * sl_ref[e, a * ROWS : (a + 1) * ROWS, :]).astype(bf16))
        gp = jnp.concatenate(gps, axis=0)
        gpf = [v.astype(f32) for v in gps]
        out = None
        for i in range(NF):
            rows = []
            for a in range(NF):
                acc = None
                for b in range(NF):
                    term = m1[e, i, a, b] * gpf[b]
                    acc = term if acc is None else acc + term
                rows.append(acc.astype(bf16))
            hi = jnp.concatenate(rows, axis=0)
            hg_ref[e, :, i * HB : (i + 1) * HB] = hi
            term = dot_t(hi, first_ref[e, i])
            out = term if out is None else out + term
        for a in range(NF):
            out_ref[e * ROWS : (e + 1) * ROWS, a * DB : (a + 1) * DB] = group(out, a).astype(bf16)
        hid = side_ref[e, :, SIDE:]
        mix2 = pair_sums([dot_t(hid, gs[i].astype(bf16)) for i in range(NF)], same, NF)
        mix1 = pair_sums([dot_t(side_ref[e, :, i * HB : (i + 1) * HB], gp) for i in range(NF)], same, 0)
        out_ref[e * ROWS : (e + 1) * ROWS, DIM:] = hi_lo(mix1 + mix2, lane < 2 * NF).astype(bf16)


def weight_grad_body(x_ref, side_ref, hg_ref, first_ref, second_ref):
    for e in range(2):
        xs = split_blocks(x_ref[e * ROWS : (e + 1) * ROWS, :DIM].astype(bf16))
        g = hg_ref[e, :, NF * HB : NF * HB + DB]
        for i in range(NF):
            first_ref[e, i] = dot_0(xs, hg_ref[e, :, i * HB : (i + 1) * HB]).astype(bf16)
            second_ref[e, i] = dot_0(g, side_ref[e, :, (NF + i) * HB : (NF + i + 1) * HB]).astype(bf16)


def combine_grad_body(parts_ref, w_ref, total_ref, grad_ref, cg_ref, cols_ref):
    out_b = sum_parts(parts_ref).astype(bf16)
    cg = dot_t(out_b, grad_ref[...])
    total = total_ref[...]
    cg_ref[:32] = cg
    cg_ref[32:] = jnp.broadcast_to(total, (8, TOK))
    cols = tile_of(jnp.sum(w_ref[:32] / total * cg, axis=0, keepdims=True))
    cols_ref[...] = jnp.broadcast_to(cols[None], cols_ref.shape)


def logit_body(p0, p1, p2, p3, cdots_ref, x_ref, w_ref, cg_ref, tok_ref, pay_ref, ug_ref, mix_ref):
    total = sum_ring(p0, p1, p2, p3)
    mix_ref[...] = total[:, DIM:]
    grad = total[:, :DIM]
    grad_b = grad.astype(bf16)
    ddot = jnp.sum(x_ref[:, :DIM] * grad, axis=1, keepdims=True)
    cdot = row_of(jnp.sum(cdots_ref[...], axis=0))
    tok = tok_ref[...]
    dg = dot_t(grad_b, tok)
    w = w_ref[:32]
    combine = w / cg_ref[32:33]
    dispatch = w / x_ref[:, DIM : DIM + 1]
    lg = combine * (cg_ref[:32] - cdot) + dispatch * (dg - ddot)
    lgb = (logit_gain * lg * w_ref[32:33]).astype(bf16)
    ug_ref[...] = dot(lgb, tok).astype(bf16)
    db = dispatch.astype(bf16)
    for k in range(STEPS):
        pay_ref[k, :, :DIM] = grad_b
        pay_ref[k, :, DIM : DIM + CHUNK] = lgb[:, chunk(k)]
        pay_ref[k, :, DIM + CHUNK :] = db[:, chunk(k)]


def token_body(place, recv_ref, s0, s1, s2, s3, tok_ref, keep_ref, send_ref):
    direct = None
    through = None
    for k, slot_ref in enumerate((s0, s1, s2, s3)):
        at = (place[0] + 4 - k) & 3
        unit_b = unit_rows(slot_ref[...].astype(f32)).astype(bf16)
        d = dot_0(recv_ref[at, :, DIM + CHUNK :], recv_ref[at, :, :DIM])
        u = dot_0(recv_ref[at, :, DIM : DIM + CHUNK], unit_b)
        direct = d if direct is None else direct + d
        through = u if through is None else through + u
    first = place[1] == 0
    for y in range(4):
        pair = []
        for c in range(2):
            lo = (y * 2 + c) * 32
            t = tok_ref[lo : lo + 32, :].astype(f32)
            u = through[lo : lo + 32]
            n2 = jnp.sum(t * t, axis=1, keepdims=True) + norm_eps
            coef = jnp.sum(t * u, axis=1, keepdims=True) / n2
            pair.append(direct[lo : lo + 32] + u - t * coef)
        keep_ref[y] = jnp.where(first, pair[0], pair[1])
        send_ref[y] = jnp.where(first, pair[1], pair[0]).astype(bf16)


def slot_body(p0, p1, slot_ref, out_ref):
    ug = p0[...].astype(f32) + p1[...].astype(f32)
    values = slot_ref[...].astype(f32)
    norm = jnp.sqrt(jnp.sum(values * values, axis=1, keepdims=True) + norm_eps)
    unit = values / norm
    out_ref[...] = (ug - unit * jnp.sum(unit * ug, axis=1, keepdims=True)) / norm


def swap(value, axis):
    return lax.ppermute(value, axis, [(0, 1), (1, 0)])


def exchange(value, axes):
    return lax.all_to_all(value, axes, 0, 0)


def ring(value, axis):
    pairs = [[(i, (i + k) % 4) for i in range(4)] for k in range(1, 4)]
    return [value] + [lax.ppermute(value, axis, p) for p in pairs]


def far_sum(value):
    return (value.astype(f32) + swap(value, "h").astype(f32)).astype(bf16)


def gather_x(value):
    return exchange(jnp.broadcast_to(value[None], (4,) + value.shape), "x")


tie = lax.optimization_barrier


def local(tokens, out_grad, slot_params, m1, first_blocks, m2, second_blocks):
    second_turned = jnp.swapaxes(second_blocks, 2, 3)
    slot_all = ring(slot_params, "z")
    w, colsum, input_part = call(
        routing_body,
        (sds((40, TOK), f32), sds((32, 8, 128), f32), sds((32, DIM + EXTRA), bf16)),
        0,
        (slot_params, tokens),
        4 * 32 * TOK * DIM,
        4 << 20,
        "routing",
        True,
    )
    input_far = far_sum(input_part)
    col_parts = exchange(colsum, exp_axes)
    col_parts, input_far, *slot_all = tie((col_parts, input_far, *slot_all))
    total, grad_part = call(
        combine_body,
        (sds((1, TOK), f32), sds((32, DIM), bf16)),
        0,
        (col_parts, w, out_grad),
        2 * 32 * TOK * DIM,
        4 << 20,
        "combine",
    )
    input_parts = ring(input_far, "x")
    grad_far = far_sum(grad_part)
    *input_parts, grad_far = tie((*input_parts, grad_far))
    grad_parts = gather_x(grad_far)
    x, side, slopes, out_part = call(
        forward_body,
        (
            sds((32, DIM + EXTRA), f32),
            sds((2, 64, SIDE + HB), bf16),
            sds((2, 64, HB), f32),
            sds((32, DIM), bf16),
        ),
        2,
        (m1, m2, *input_parts, first_blocks, second_turned),
        4 * 128 * 1024 * DB,
        5 << 20,
        "forward",
    )
    out_far = far_sum(out_part)
    hg, input_grad_part = call(
        backward_body,
        (sds((2, 64, NF * HB + 512), bf16), sds((32, DIM + EXTRA), bf16)),
        2,
        (m1, m2, grad_parts, first_blocks, second_turned, side, slopes),
        4 * 128 * 1024 * DB,
        5 << 20,
        "backward",
    )
    out_parts = gather_x(out_far)
    input_grad_far = far_sum(input_grad_part)
    out_parts, input_grad_far = tie((out_parts, input_grad_far))
    input_grad_parts = ring(input_grad_far, "x")
    cg, cols = call(
        combine_grad_body,
        (sds((40, TOK), f32), sds((32, 8, 128), f32)),
        0,
        (out_parts, w, total, out_grad),
        2 * 32 * TOK * DIM,
        4 << 20,
        "combine_grad",
    )
    cdots = exchange(cols, exp_axes)
    pay, ug_part, mix = call(
        logit_body,
        (sds((4, 32, DIM + 512), bf16), sds((32, DIM), bf16), sds((32, EXTRA), f32)),
        0,
        (*input_grad_parts, cdots, x, w, cg, tokens),
        4 * 32 * TOK * DIM,
        4 << 20,
        "logit_grad",
    )
    first_grad, second_grad = call(
        weight_grad_body,
        (sds(first_blocks.shape, bf16), sds(second_turned.shape, bf16)),
        0,
        (x, side, hg),
        4 * 128 * 1024 * DB,
        5 << 20,
        "weight_grad",
    )
    recv = exchange(pay, "z")
    u0, u1, u2, u3 = (u.astype(f32) for u in ring(ug_part, "x"))
    ug_near = ((u0 + u2) + (u1 + u3)).astype(bf16)
    recv, ug_near = tie((recv, ug_near))
    ug_parts = (ug_near, swap(ug_near, "h"))
    quarter = lax.dynamic_slice_in_dim(tokens, lax.axis_index("z") * 256, 256, 0)
    place = jnp.stack([lax.axis_index("z"), lax.axis_index("c")]).astype(jnp.int32)
    keep, send = call(
        token_body,
        (sds((4, 32, DIM), f32), sds((4, 32, DIM), bf16)),
        1,
        (place, recv, *slot_all, quarter),
        4 * 128 * 256 * DIM,
        4 << 20,
        "token_grad",
    )
    half = (keep + swap(send, "c").astype(f32)).astype(bf16)
    grad_tokens = jnp.sum(exchange(half, "y").astype(f32), axis=0)
    grad_slots = call(
        slot_body, sds((32, DIM), f32), 0, (*ug_parts, slot_params), 32 * DIM * 8, 1 << 20, "slot_grad"
    )
    mixes = (mix[:, : 2 * NF] + mix[:, 2 * NF : 4 * NF]).reshape(2, NF, NF, 2, NF)
    return (
        grad_tokens,
        grad_slots,
        mixes[:, :, :, 0],
        first_grad,
        mixes[:, :, :, 1],
        jnp.swapaxes(second_grad, 2, 3),
    )


def solution(mesh):
    fine = Mesh(mesh.devices.reshape(2, 4, 4, 4, 2), seq_axes + exp_axes)
    return jax.shard_map(
        local,
        mesh=fine,
        in_specs=(
            P(seq_axes, None),
            P(seq_axes, None),
            P(exp_axes, None),
            P(exp_axes, None, None, None),
            P(exp_axes, None, None, seq_axes),
            P(exp_axes, None, None, None),
            P(exp_axes, None, seq_axes, None),
        ),
        out_specs=(
            P(seq_axes + exp_axes, None),
            P(exp_axes, None),
            P(exp_axes, None, None, None),
            P(exp_axes, None, None, seq_axes),
            P(exp_axes, None, None, None),
            P(exp_axes, None, seq_axes, None),
        ),
        check_vma=False,
    )
```

```python
import jax
import jax.numpy as jnp
from jax import lax
from jax.experimental import pallas as pl
from jax.experimental.pallas import tpu as pltpu
from jax.sharding import Mesh, PartitionSpec as P

logit_gain = 64.0
norm_eps = 1e-06
gelu_coef = 0.7978845608028654
cubic_coef = 0.044715

f32 = jnp.float32
bf16 = jnp.bfloat16
DIM = 1664
EXTRA = 128
DB = 416
NF = 4
ROWS = 16
HB = 256
TOK = 1024
CHUNK = 256
STEPS = TOK // CHUNK
WIDE = 60 << 20
SMALL = 51 << 20
SIDE = 2 * NF * HB
VMEM = pltpu.VMEM
SMEM = pltpu.SMEM
seq_axes = ("h", "x")
exp_axes = ("z", "y", "c")


def dot(a, b):
    return jnp.dot(a, b, preferred_element_type=f32)


def dot_t(a, b):
    return lax.dot_general(a, b, (((1,), (1,)), ((), ())), preferred_element_type=f32)


def dot_0(a, b):
    return lax.dot_general(a, b, (((0,), (0,)), ((), ())), preferred_element_type=f32)


def call(body, out, n_smem, args, flops, byts, name, streamed=False):
    ins = [pl.BlockSpec(memory_space=VMEM)] * (len(args) - n_smem)
    scratch = []
    if streamed:
        ins[-1] = pl.BlockSpec(memory_space=pl.ANY)
        scratch = [VMEM(args[-1].shape, args[-1].dtype), pltpu.SemaphoreType.DMA((STEPS,))]
    return pl.pallas_call(
        body,
        out_shape=out,
        in_specs=[pl.BlockSpec(memory_space=SMEM)] * n_smem + ins,
        out_specs=jax.tree.map(lambda o: pl.BlockSpec(memory_space=VMEM), out),
        scratch_shapes=scratch,
        compiler_params=pltpu.CompilerParams(vmem_limit_bytes=WIDE if streamed else SMALL),
        cost_estimate=pl.CostEstimate(flops=flops, bytes_accessed=byts, transcendentals=0),
        name=name,
    )(*args)


def stream(source, target, sems):
    copies = []
    for k in range(STEPS):
        rows = pl.ds(k * CHUNK, CHUNK)
        copies.append(pltpu.make_async_copy(source.at[rows], target.at[rows], sems.at[k]))
        copies[-1].start()
    return copies


def chunk(k):
    return slice(k * CHUNK, (k + 1) * CHUNK)


def sds(shape, dtype):
    return jax.ShapeDtypeStruct(shape, dtype)


def unit_rows(values):
    norm = jnp.sqrt(jnp.sum(values * values, axis=1, keepdims=True) + norm_eps)
    return values / norm


def hi_lo(value, first):
    hi = value.astype(bf16).astype(f32)
    return jnp.where(first, hi, value - hi)


def split_blocks(rows):
    return jnp.concatenate([rows[:, a * DB : (a + 1) * DB] for a in range(NF)], axis=0)


def group(rows, a):
    return rows[a * ROWS : (a + 1) * ROWS]


def routing_body(slot_ref, tok_hbm, w_ref, colsum_ref, pay_ref, tok_ref, sems):
    copies = stream(tok_hbm, tok_ref, sems)
    unit_b = unit_rows(slot_ref[...].astype(f32)).astype(bf16)
    acc = jnp.zeros(slot_ref.shape, f32)
    total = jnp.zeros((slot_ref.shape[0], 1), f32)
    tiles = []
    for k in range(STEPS):
        copies[k].wait()
        inv = []
        for r in range(CHUNK // 128):
            part = tok_ref[k * CHUNK + r * 128 : k * CHUNK + (r + 1) * 128, :].astype(f32)
            sq = jnp.sum(part * part, axis=1, keepdims=True)
            inv.append(jnp.transpose(jnp.broadcast_to(sq, (128, 128)))[0:1])
        inv = lax.rsqrt(jnp.concatenate(inv, axis=1) + norm_eps)
        cols = chunk(k)
        w_ref[32:, cols] = jnp.broadcast_to(inv, (8, CHUNK))
        tok = tok_ref[cols, :]
        w = jnp.exp(logit_gain * dot_t(unit_b, tok) * inv)
        w_ref[:32, cols] = w
        sums = jnp.sum(w, axis=0, keepdims=True)
        tiles += [sums[:, r * 128 : (r + 1) * 128] for r in range(CHUNK // 128)]
        acc = acc + dot(w.astype(bf16), tok)
        total = total + jnp.sum(w, axis=1, keepdims=True)
    wide = jnp.broadcast_to(total, (total.shape[0], EXTRA))
    lane = lax.broadcasted_iota(jnp.int32, wide.shape, 1)
    pay_ref[:, :DIM] = acc.astype(bf16)
    pay_ref[:, DIM:] = hi_lo(wide, lane < 1).astype(bf16)
    cols = jnp.concatenate(tiles, axis=0)
    colsum_ref[...] = jnp.broadcast_to(cols[None], colsum_ref.shape)


def row_of(tile):
    return jnp.concatenate([tile[r : r + 1] for r in range(8)], axis=1)


def tile_of(row):
    return jnp.concatenate([row[:, r * 128 : (r + 1) * 128] for r in range(8)], axis=0)


def combine_body(parts_ref, w_ref, grad_ref, total_ref, out_ref):
    total = row_of(jnp.sum(parts_ref[...], axis=0))
    total_ref[...] = total
    combine = (w_ref[:32] / total).astype(bf16)
    out_ref[...] = dot(combine, grad_ref[...]).astype(bf16)


def sum_parts(ref):
    total = ref[0].astype(f32)
    for k in range(1, ref.shape[0]):
        total = total + ref[k].astype(f32)
    return total


def sum_ring(a, b, c, d):
    return (a[...].astype(f32) + c[...].astype(f32)) + (b[...].astype(f32) + d[...].astype(f32))


def forward_body(m1, m2, p0, p1, p2, p3, first_ref, second_ref, x_ref, side_ref, sl_ref, out_ref):
    total = sum_ring(p0, p1, p2, p3)
    dt = total[:, DIM : DIM + 1] + total[:, DIM + 1 : DIM + 2]
    x_ref[:, DIM:] = jnp.broadcast_to(dt, (dt.shape[0], EXTRA))
    x = total[:, :DIM] / dt
    x_ref[:, :DIM] = x
    xb = x.astype(bf16)
    for e in range(2):
        xs = split_blocks(xb[e * ROWS : (e + 1) * ROWS])
        ys = [dot(xs, first_ref[e, i]) for i in range(NF)]
        for i in range(NF):
            side_ref[e, :, i * HB : (i + 1) * HB] = ys[i].astype(bf16)
        hid = []
        for b in range(NF):
            pre = None
            for i in range(NF):
                for a in range(NF):
                    term = m1[e, i, a, b] * group(ys[i], a)
                    pre = term if pre is None else pre + term
            inner = gelu_coef * (pre + cubic_coef * pre * pre * pre)
            tang = jnp.tanh(inner)
            hid_b = (0.5 * pre * (1.0 + tang)).astype(bf16)
            side_ref[e, b * ROWS : (b + 1) * ROWS, SIDE:] = hid_b
            hid.append(hid_b.astype(f32))
            sl_ref[e, b * ROWS : (b + 1) * ROWS, :] = 0.5 * (1.0 + tang) + 0.5 * pre * (
                1.0 - tang * tang
            ) * gelu_coef * (1.0 + 3.0 * cubic_coef * pre * pre)
        out = None
        for i in range(NF):
            rows = []
            for b in range(NF):
                acc = None
                for a in range(NF):
                    term = m2[e, i, a, b] * hid[a]
                    acc = term if acc is None else acc + term
                rows.append(acc.astype(bf16))
            si = jnp.concatenate(rows, axis=0)
            side_ref[e, :, (NF + i) * HB : (NF + i + 1) * HB] = si
            term = dot_t(si, second_ref[e, i])
            out = term if out is None else out + term
        for b in range(NF):
            out_ref[e * ROWS : (e + 1) * ROWS, b * DB : (b + 1) * DB] = group(out, b).astype(bf16)


def pair_sums(mats, same, column):
    rows = []
    for mat in mats:
        masked = jnp.where(same, mat, 0.0)
        for a in range(NF):
            rows.append(jnp.sum(group(masked, a), axis=0, keepdims=True))
    stack = jnp.concatenate(rows, axis=0)
    lane = lax.broadcasted_iota(jnp.int32, (NF * NF, EXTRA), 1)
    result = jnp.zeros((NF * NF, EXTRA), f32)
    for b in range(NF):
        value = jnp.sum(stack[:, b * ROWS : (b + 1) * ROWS], axis=1, keepdims=True)
        here = (lane == column + b) | (lane == column + b + 2 * NF)
        result = jnp.where(here, value, result)
    return result


def backward_body(m1, m2, parts_ref, first_ref, second_ref, side_ref, sl_ref, hg_ref, out_ref):
    grad_b = sum_parts(parts_ref).astype(bf16)
    n = NF * ROWS
    r = lax.broadcasted_iota(jnp.int32, (n, n), 0)
    c = lax.broadcasted_iota(jnp.int32, (n, n), 1)
    same = (r & (ROWS - 1)) == (c & (ROWS - 1))
    lane = lax.broadcasted_iota(jnp.int32, (NF * NF, EXTRA), 1)
    for e in range(2):
        g = split_blocks(grad_b[e * ROWS : (e + 1) * ROWS])
        hg_ref[e, :, NF * HB : NF * HB + DB] = g
        gs = [dot(g, second_ref[e, i]) for i in range(NF)]
        gps = []
        for a in range(NF):
            acc = None
            for i in range(NF):
                for b in range(NF):
                    term = m2[e, i, a, b] * group(gs[i], b)
                    acc = term if acc is None else acc + term
            gps.append((acc * sl_ref[e, a * ROWS : (a + 1) * ROWS, :]).astype(bf16))
        gp = jnp.concatenate(gps, axis=0)
        gpf = [v.astype(f32) for v in gps]
        out = None
        for i in range(NF):
            rows = []
            for a in range(NF):
                acc = None
                for b in range(NF):
                    term = m1[e, i, a, b] * gpf[b]
                    acc = term if acc is None else acc + term
                rows.append(acc.astype(bf16))
            hi = jnp.concatenate(rows, axis=0)
            hg_ref[e, :, i * HB : (i + 1) * HB] = hi
            term = dot_t(hi, first_ref[e, i])
            out = term if out is None else out + term
        for a in range(NF):
            out_ref[e * ROWS : (e + 1) * ROWS, a * DB : (a + 1) * DB] = group(out, a).astype(bf16)
        hid = side_ref[e, :, SIDE:]
        mix2 = pair_sums([dot_t(hid, gs[i].astype(bf16)) for i in range(NF)], same, NF)
        mix1 = pair_sums([dot_t(side_ref[e, :, i * HB : (i + 1) * HB], gp) for i in range(NF)], same, 0)
        out_ref[e * ROWS : (e + 1) * ROWS, DIM:] = hi_lo(mix1 + mix2, lane < 2 * NF).astype(bf16)


def weight_grad_body(x_ref, side_ref, hg_ref, first_ref, second_ref):
    for e in range(2):
        xs = split_blocks(x_ref[e * ROWS : (e + 1) * ROWS, :DIM].astype(bf16))
        g = hg_ref[e, :, NF * HB : NF * HB + DB]
        for i in range(NF):
            first_ref[e, i] = dot_0(xs, hg_ref[e, :, i * HB : (i + 1) * HB]).astype(bf16)
            second_ref[e, i] = dot_0(g, side_ref[e, :, (NF + i) * HB : (NF + i + 1) * HB]).astype(bf16)


def combine_grad_body(parts_ref, w_ref, total_ref, grad_ref, cg_ref, cols_ref):
    out_b = sum_parts(parts_ref).astype(bf16)
    cg = dot_t(out_b, grad_ref[...])
    total = total_ref[...]
    cg_ref[:32] = cg
    cg_ref[32:] = jnp.broadcast_to(total, (8, TOK))
    cols = tile_of(jnp.sum(w_ref[:32] / total * cg, axis=0, keepdims=True))
    cols_ref[...] = jnp.broadcast_to(cols[None], cols_ref.shape)


def logit_body(p0, p1, p2, p3, cdots_ref, x_ref, w_ref, cg_ref, tok_ref, pay_ref, ug_ref, mix_ref):
    total = sum_ring(p0, p1, p2, p3)
    mix_ref[...] = total[:, DIM:]
    grad = total[:, :DIM]
    grad_b = grad.astype(bf16)
    ddot = jnp.sum(x_ref[:, :DIM] * grad, axis=1, keepdims=True)
    cdot = row_of(jnp.sum(cdots_ref[...], axis=0))
    tok = tok_ref[...]
    dg = dot_t(grad_b, tok)
    w = w_ref[:32]
    combine = w / cg_ref[32:33]
    dispatch = w / x_ref[:, DIM : DIM + 1]
    lg = combine * (cg_ref[:32] - cdot) + dispatch * (dg - ddot)
    lgb = (logit_gain * lg * w_ref[32:33]).astype(bf16)
    ug_ref[...] = dot(lgb, tok).astype(bf16)
    db = dispatch.astype(bf16)
    for k in range(STEPS):
        pay_ref[k, :, :DIM] = grad_b
        pay_ref[k, :, DIM : DIM + CHUNK] = lgb[:, chunk(k)]
        pay_ref[k, :, DIM + CHUNK :] = db[:, chunk(k)]


def token_body(place, recv_ref, s0, s1, s2, s3, tok_ref, keep_ref, send_ref):
    direct = None
    through = None
    for k, slot_ref in enumerate((s0, s1, s2, s3)):
        at = (place[0] + 4 - k) & 3
        unit_b = unit_rows(slot_ref[...].astype(f32)).astype(bf16)
        d = dot_0(recv_ref[at, :, DIM + CHUNK :], recv_ref[at, :, :DIM])
        u = dot_0(recv_ref[at, :, DIM : DIM + CHUNK], unit_b)
        direct = d if direct is None else direct + d
        through = u if through is None else through + u
    first = place[1] == 0
    for y in range(4):
        pair = []
        for c in range(2):
            lo = (y * 2 + c) * 32
            t = tok_ref[lo : lo + 32, :].astype(f32)
            u = through[lo : lo + 32]
            n2 = jnp.sum(t * t, axis=1, keepdims=True) + norm_eps
            coef = jnp.sum(t * u, axis=1, keepdims=True) / n2
            pair.append(direct[lo : lo + 32] + u - t * coef)
        keep_ref[y] = jnp.where(first, pair[0], pair[1])
        send_ref[y] = jnp.where(first, pair[1], pair[0]).astype(bf16)


def slot_body(p0, p1, slot_ref, out_ref):
    ug = p0[...].astype(f32) + p1[...].astype(f32)
    values = slot_ref[...].astype(f32)
    norm = jnp.sqrt(jnp.sum(values * values, axis=1, keepdims=True) + norm_eps)
    unit = values / norm
    out_ref[...] = (ug - unit * jnp.sum(unit * ug, axis=1, keepdims=True)) / norm


def swap(value, axis):
    return lax.ppermute(value, axis, [(0, 1), (1, 0)])


def exchange(value, axes):
    return lax.all_to_all(value, axes, 0, 0)


def ring(value, axis):
    pairs = [[(i, (i + k) % 4) for i in range(4)] for k in range(1, 4)]
    return [value] + [lax.ppermute(value, axis, p) for p in pairs]


def far_sum(value):
    return (value.astype(f32) + swap(value, "h").astype(f32)).astype(bf16)


def gather_x(value):
    return exchange(jnp.broadcast_to(value[None], (4,) + value.shape), "x")


tie = lax.optimization_barrier


def local(tokens, out_grad, slot_params, m1, first_blocks, m2, second_blocks):
    second_turned = jnp.swapaxes(second_blocks, 2, 3)
    w, colsum, input_part = call(
        routing_body,
        (sds((40, TOK), f32), sds((32, 8, 128), f32), sds((32, DIM + EXTRA), bf16)),
        0,
        (slot_params, tokens),
        4 * 32 * TOK * DIM,
        4 << 20,
        "routing",
        True,
    )
    input_far = far_sum(input_part)
    col_parts = exchange(colsum, exp_axes)
    col_parts, input_far = tie((col_parts, input_far))
    total, grad_part = call(
        combine_body,
        (sds((1, TOK), f32), sds((32, DIM), bf16)),
        0,
        (col_parts, w, out_grad),
        2 * 32 * TOK * DIM,
        4 << 20,
        "combine",
    )
    input_parts = ring(input_far, "x")
    grad_far = far_sum(grad_part)
    *input_parts, grad_far = tie((*input_parts, grad_far))
    grad_parts = gather_x(grad_far)
    x, side, slopes, out_part = call(
        forward_body,
        (
            sds((32, DIM + EXTRA), f32),
            sds((2, 64, SIDE + HB), bf16),
            sds((2, 64, HB), f32),
            sds((32, DIM), bf16),
        ),
        2,
        (m1, m2, *input_parts, first_blocks, second_turned),
        4 * 128 * 1024 * DB,
        5 << 20,
        "forward",
    )
    out_far = far_sum(out_part)
    hg, input_grad_part = call(
        backward_body,
        (sds((2, 64, NF * HB + 512), bf16), sds((32, DIM + EXTRA), bf16)),
        2,
        (m1, m2, grad_parts, first_blocks, second_turned, side, slopes),
        4 * 128 * 1024 * DB,
        5 << 20,
        "backward",
    )
    out_parts = gather_x(out_far)
    input_grad_far = far_sum(input_grad_part)
    out_parts, input_grad_far = tie((out_parts, input_grad_far))
    input_grad_parts = ring(input_grad_far, "x")
    out_parts, slot_own = tie((out_parts, slot_params))
    slot_all = ring(slot_own, "z")
    *input_grad_parts, s1, s2, s3 = tie((*input_grad_parts, *slot_all[1:]))
    slot_all = (slot_params, s1, s2, s3)
    cg, cols = call(
        combine_grad_body,
        (sds((40, TOK), f32), sds((32, 8, 128), f32)),
        0,
        (out_parts, w, total, out_grad),
        2 * 32 * TOK * DIM,
        4 << 20,
        "combine_grad",
    )
    cdots = exchange(cols, exp_axes)
    pay, ug_part, mix = call(
        logit_body,
        (sds((4, 32, DIM + 512), bf16), sds((32, DIM), bf16), sds((32, EXTRA), f32)),
        0,
        (*input_grad_parts, cdots, x, w, cg, tokens),
        4 * 32 * TOK * DIM,
        4 << 20,
        "logit_grad",
    )
    first_grad, second_grad = call(
        weight_grad_body,
        (sds(first_blocks.shape, bf16), sds(second_turned.shape, bf16)),
        0,
        (x, side, hg),
        4 * 128 * 1024 * DB,
        5 << 20,
        "weight_grad",
    )
    recv = exchange(pay, "z")
    u0, u1, u2, u3 = (u.astype(f32) for u in ring(ug_part, "x"))
    ug_near = ((u0 + u2) + (u1 + u3)).astype(bf16)
    recv, ug_near = tie((recv, ug_near))
    ug_parts = (ug_near, swap(ug_near, "h"))
    quarter = lax.dynamic_slice_in_dim(tokens, lax.axis_index("z") * 256, 256, 0)
    place = jnp.stack([lax.axis_index("z"), lax.axis_index("c")]).astype(jnp.int32)
    keep, send = call(
        token_body,
        (sds((4, 32, DIM), f32), sds((4, 32, DIM), bf16)),
        1,
        (place, recv, *slot_all, quarter),
        4 * 128 * 256 * DIM,
        4 << 20,
        "token_grad",
    )
    half = (keep + swap(send, "c").astype(f32)).astype(bf16)
    grad_tokens = jnp.sum(exchange(half, "y").astype(f32), axis=0)
    grad_slots = call(
        slot_body, sds((32, DIM), f32), 0, (*ug_parts, slot_params), 32 * DIM * 8, 1 << 20, "slot_grad"
    )
    mixes = (mix[:, : 2 * NF] + mix[:, 2 * NF : 4 * NF]).reshape(2, NF, NF, 2, NF)
    return (
        grad_tokens,
        grad_slots,
        mixes[:, :, :, 0],
        first_grad,
        mixes[:, :, :, 1],
        jnp.swapaxes(second_grad, 2, 3),
    )


def solution(mesh):
    fine = Mesh(mesh.devices.reshape(2, 4, 4, 4, 2), seq_axes + exp_axes)
    return jax.shard_map(
        local,
        mesh=fine,
        in_specs=(
            P(seq_axes, None),
            P(seq_axes, None),
            P(exp_axes, None),
            P(exp_axes, None, None, None),
            P(exp_axes, None, None, seq_axes),
            P(exp_axes, None, None, None),
            P(exp_axes, None, seq_axes, None),
        ),
        out_specs=(
            P(seq_axes + exp_axes, None),
            P(exp_axes, None),
            P(exp_axes, None, None, None),
            P(exp_axes, None, None, seq_axes),
            P(exp_axes, None, None, None),
            P(exp_axes, None, seq_axes, None),
        ),
        check_vma=False,
    )
```
